256 devices in a mesh: row: 8 (over y, z_lo), col: 32 (over x, z_hi, core).
Axes of the slice: x: 4, y: 4, z: 8 (z_hi: 4, z_lo: 2; z = z_hi * 2 + z_lo), core: 2. Of those that a mesh axis runs over, the one named last changes fastest.
Arguments:
- features: bfloat16 [32768, 128], P(('col', 'row')), may hold values from -6 to 6
- weight: bfloat16 [128, 256], replicated, may hold values from -0.5 to 0.5
- history: bfloat16 [32768, 256], P(('col', 'row')), may hold values from -6 to 6
- in_batch: int32 [32768], P(('col', 'row')), may hold values 0 or 1
- tile_values: bfloat16 [8, 32, 192, 128, 128], P('row', 'col'), as said below
- tile_pos: int32 [8, 32, 192, 2], P('row', 'col'), may hold values from 0 to 31, as said below
- tile_count: int32 [8, 32], P('row', 'col'), may hold values from 1 to 192, as said below
- cotangent: bfloat16 [32768, 256], P(('row', 'col')), may hold values from -6 to 6
Outputs:
- output: bfloat16 [32768, 256], P(('row', 'col'))
- grad_features: bfloat16 [32768, 128], P(('col', 'row'))
- grad_weight: float32 [128, 256], replicated
The draws below stay inside these ranges and needn't reach their ends.
Inputs may be any that keep to these rules, and one draw needn't show every extreme that they name: tile_pos[..., 0] lies in 0 to 128 * 32 / 128 - 1 and tile_pos[..., 1] in 0 to 128 * 8 / 128 - 1. `tile_count`: at least one block uses all 192 slots. `tile_values`: entries are nonnegative.
All inputs are finite; a program needn't handle non-finite values. No bound on the sum of `in_batch` on one device may be relied on, other than what follows from the above.
Results may differ from the reference program's by a relative error of at most 0.006.
Values may be sent and summed in bfloat16 or wider, within the bound.
No kernel may reach another device: no remote copies, remote signals or barrier semaphores. Data moves between devices by JAX's collectives and lax.ppermute only.
A program may use at most 128 MiB of HBM per device.

```python
import jax
import jax.numpy as jnp
from jax import lax

FIN = 128
HID = 256
EDGE = 128
NODE_DEV = 128
TILES = 192
NODES = 32768
N_ROW = 8
N_COL = 32


def draw_tile_values(key, part):
    key_mask = jax.random.fold_in(key, 31)
    key_size = jax.random.fold_in(key, 32)
    shape = (N_ROW, N_COL, TILES, EDGE, EDGE)
    present = (jax.random.randint(key_mask, shape, 0, 4, dtype=jnp.int32) == 0).astype(jnp.float32)
    sizes = jax.random.uniform(key_size, shape, jnp.float32, 0.5, 1.5)
    scale = (TILES * 2048 / NODE_DEV) ** (-0.5)
    return (present * sizes * jnp.float32(scale)).astype(jnp.bfloat16)


def draw_tile_pos(key, part):
    key_rows = jax.random.fold_in(key, 11)
    key_cols = jax.random.fold_in(key, 12)
    tile_rows = jax.random.randint(key_rows, (N_ROW, N_COL, TILES), 0, NODE_DEV * N_COL // 128, dtype=jnp.int32)
    tile_cols = jax.random.randint(key_cols, (N_ROW, N_COL, TILES), 0, NODE_DEV * N_ROW // 128, dtype=jnp.int32)
    return jnp.stack([tile_rows, tile_cols], axis=-1)


def draw_tile_count(key, part):
    key_shift = jax.random.fold_in(key, 21)
    key_full = jax.random.fold_in(key, 22)
    shifts = jax.random.randint(key_shift, (N_ROW, N_COL), 0, 4, dtype=jnp.int32)
    counts = jnp.maximum(jnp.right_shift(jnp.int32(TILES), shifts), 1)
    chosen = jax.random.randint(key_full, (), 0, N_ROW * N_COL, dtype=jnp.int32)
    flat_ids = jnp.arange(N_ROW * N_COL, dtype=jnp.int32).reshape(N_ROW, N_COL)
    return jnp.where(flat_ids == chosen, jnp.int32(TILES), counts).astype(jnp.int32)


def touch_ends(drawn, rng, smallest, largest):
    extent = drawn.shape
    place = [jax.random.randint(jax.random.fold_in(rng, axis), (), 0, extent[axis]) for axis in range(len(extent))]
    drawn = drawn.at[tuple(place)].set(smallest)
    longest = extent.index(max(extent))
    place[longest] = (place[longest] + 1) % extent[longest]
    return drawn.at[tuple(place)].set(largest)


def shard_levels(rng, extent, split, low, largest):
    gain, own = 1.0, jax.random.fold_in(rng, 6)
    for axis_at, blocks in split:
        draws = jnp.exp(jax.random.uniform(jax.random.fold_in(own, axis_at), (blocks,), jnp.float32, low / len(split), largest / len(split)))
        gain = gain * jnp.repeat(draws, extent[axis_at] // blocks).reshape([-1 if axis == axis_at else 1 for axis in range(len(extent))])
    return gain


def normal_values(key, extent, width, most, cuts=(), held_as=jnp.bfloat16):
    level = shard_levels(key, extent, cuts, -0.22, 0.18) if cuts else 1.0
    entries = jax.random.normal(key, extent, jnp.float32) * width * level
    return jnp.minimum(jnp.maximum(entries, -most), most).astype(held_as)


def setup_inputs(seed: int = 0) -> dict:
    splits = jax.random.split(jax.random.key(seed), 9)
    return {
        "features": normal_values(splits[0], (NODES, FIN), 1.0, 6.0, ((0, 256),)),
        "weight": normal_values(splits[1], (FIN, HID), FIN ** -0.5, 0.5),
        "history": normal_values(splits[2], (NODES, HID), 1.0, 6.0, ((0, 256),)),
        "in_batch": touch_ends((jax.random.randint(splits[3], (NODES,), 0, 2) < 1).astype(jnp.int32), jax.random.fold_in(splits[3], 1), 0, 1),
        "tile_values": draw_tile_values(jax.random.fold_in(splits[8], 71), 0),
        "tile_pos": draw_tile_pos(jax.random.fold_in(splits[8], 71), 0),
        "tile_count": draw_tile_count(jax.random.fold_in(splits[8], 71), 0),
        "cotangent": normal_values(splits[7], (NODES, HID), 1.0, 6.0, ((0, 256),)),
    }


def gelu_form(values):
    return jax.nn.gelu(values, approximate=True)

def reference(features, weight, history, in_batch, tile_values, tile_pos, tile_count, cotangent):
    block_rows = NODE_DEV * N_COL
    block_cols = NODE_DEV * N_ROW
    projected = jnp.dot(features, weight, preferred_element_type=jnp.float32).astype(jnp.bfloat16)
    mixed = jnp.where(in_batch[:, None] == 1, projected, history)
    slot_ids = jnp.arange(TILES, dtype=jnp.int32)

    def block_parts(index):
        brow = (index // N_COL).astype(jnp.int32)
        bcol = (index % N_COL).astype(jnp.int32)
        tiles = tile_values[brow, bcol].astype(jnp.float32)
        coords = tile_pos[brow, bcol]
        valid = (slot_ids < tile_count[brow, bcol]).astype(jnp.float32)
        return (brow, bcol, tiles, coords, valid)

    def forward_block(running, index):
        brow, bcol, tiles, coords, valid = block_parts(index)
        panel = lax.dynamic_slice_in_dim(mixed, (bcol * block_cols).astype(jnp.int32), block_cols, 0)
        panel_tiles = panel.reshape(block_cols // 128, 128, HID).astype(jnp.float32)[coords[:, 1]]
        product = jnp.einsum('tij,tjh->tih', tiles, panel_tiles) * valid[:, None, None]
        summed = jax.ops.segment_sum(product, coords[:, 0], num_segments=block_rows // 128)
        start = (brow * block_rows).astype(jnp.int32)
        current = lax.dynamic_slice_in_dim(running, start, block_rows, 0)
        running = lax.dynamic_update_slice_in_dim(running, current + summed.reshape(block_rows, HID), start, 0)
        return (running, None)
    total, _ = lax.scan(forward_block, jnp.zeros((NODES, HID), jnp.float32), jnp.arange(N_ROW * N_COL, dtype=jnp.int32))
    output = gelu_form(total).astype(jnp.bfloat16)
    _, pullback = jax.vjp(gelu_form, total)
    grad_total = pullback(cotangent.astype(jnp.float32))[0].astype(jnp.bfloat16)

    def backward_block(running, index):
        brow, bcol, tiles, coords, valid = block_parts(index)
        rows_here = lax.dynamic_slice_in_dim(grad_total, (brow * block_rows).astype(jnp.int32), block_rows, 0)
        grad_tiles = rows_here.reshape(block_rows // 128, 128, HID).astype(jnp.float32)[coords[:, 0]]
        product = jnp.einsum('tij,tih->tjh', tiles, grad_tiles) * valid[:, None, None]
        summed = jax.ops.segment_sum(product, coords[:, 1], num_segments=block_cols // 128)
        start = (bcol * block_cols).astype(jnp.int32)
        current = lax.dynamic_slice_in_dim(running, start, block_cols, 0)
        running = lax.dynamic_update_slice_in_dim(running, current + summed.reshape(block_cols, HID), start, 0)
        return (running, None)
    grad_mixed, _ = lax.scan(backward_block, jnp.zeros((NODES, HID), jnp.float32), jnp.arange(N_ROW * N_COL, dtype=jnp.int32))
    grad_projected = (grad_mixed * in_batch[:, None].astype(jnp.float32)).astype(jnp.bfloat16)
    grad_features = jnp.dot(grad_projected, weight.T, preferred_element_type=jnp.float32).astype(jnp.bfloat16)
    grad_weight = jnp.dot(features.T, grad_projected, preferred_element_type=jnp.float32) / jnp.sqrt(jnp.float32(NODES))
    return (output, grad_features, grad_weight)
```

```python
import math

import jax
import jax.numpy as jnp
from jax import lax
from jax.experimental import pallas as pl
from jax.experimental.pallas import tpu as pltpu
from jax.sharding import PartitionSpec as P

BF = jnp.bfloat16
F32 = jnp.float32
E = 128


def gelu_form(values):
    return jax.nn.gelu(values, approximate=True)


def col_perm(axis, step):
    pairs = []
    for dev in range(32):
        x, z, core = dev >> 3, (dev >> 1) & 3, dev & 1
        if axis == "x":
            x = (x + step) & 3
        elif axis == "z":
            z = (z + step) & 3
        else:
            core = core ^ 1
        pairs.append((dev, x * 8 + z * 2 + core))
    return pairs


def row_perm(axis, step):
    pairs = []
    for dev in range(8):
        y, half = dev >> 1, dev & 1
        if axis == "y":
            y = (y + step) & 3
        else:
            half = half ^ 1
        pairs.append((dev, y * 2 + half))
    return pairs


def shift(value, axis, step=1):
    if axis in ("x", "z", "core"):
        return lax.ppermute(value, "col", col_perm(axis, step))
    return lax.ppermute(value, "row", row_perm(axis, step))


def xor_col(value, mask):
    return lax.ppermute(value, "col", [(dev, dev ^ mask) for dev in range(32)])


def xor_row(value, mask):
    return lax.ppermute(value, "row", [(dev, dev ^ mask) for dev in range(8)])


def gather_ring(own, axis):
    half = own.shape[0] // 2
    after = shift(own, axis, -1)
    before = shift(own, axis, 1)
    far_a = shift(before[:half], axis, 1)
    far_b = shift(after[half:], axis, -1)
    return [own, after, jnp.concatenate([far_a, far_b]), before]


def reduce_ring(chunks, axis):
    half = chunks[2].shape[0] // 2
    far = chunks[2].astype(BF)
    got_a = shift(far[:half], axis, 1)
    got_b = shift(far[half:], axis, -1)
    low = (chunks[1][:half].astype(F32) + got_a.astype(F32)).astype(BF)
    high = (chunks[3][half:].astype(F32) + got_b.astype(F32)).astype(BF)
    near = shift(jnp.concatenate([low, chunks[1][half:].astype(BF)]), axis, 1)
    back = shift(jnp.concatenate([chunks[3][:half].astype(BF), high]), axis, -1)
    return chunks[0].astype(F32) + near.astype(F32) + back.astype(F32)


def dense_kernel(slots, cells, where_ref, tiles_hbm, low_ref, high_ref, tiles, head, link, sem):
    step = pl.program_id(0)

    @pl.when(step == 0)
    def _():
        copy = pltpu.make_async_copy(tiles_hbm, tiles, sem)
        copy.start()

        def clear(i, carry):
            head[i] = -1
            return carry

        lax.fori_loop(0, cells + 1, clear, 0)

        def insert(s, carry):
            at = where_ref[s]
            link[s] = head[at]
            head[at] = s
            return carry

        lax.fori_loop(0, slots, insert, 0)
        copy.wait()

    for out_ref, base in ((low_ref, 0), (high_ref, cells // 2)):
        for c in range(8):
            first = head[base + step * 8 + c]
            cols = pl.ds(c * E, E)

            @pl.when(first < 0)
            def _(out_ref=out_ref, cols=cols):
                out_ref[:, cols] = jnp.zeros((E, E), BF)

            @pl.when(first >= 0)
            def _(out_ref=out_ref, cols=cols, first=first):
                second = link[first]

                @pl.when(second < 0)
                def _():
                    out_ref[:, cols] = tiles[first]

                @pl.when(second >= 0)
                def _():
                    def more(state):
                        return state[0] >= 0

                    def add(state):
                        at, acc = state
                        return link[at], acc + tiles[at].astype(F32)

                    _, acc = lax.while_loop(more, add, (second, tiles[first].astype(F32)))
                    out_ref[:, cols] = acc.astype(BF)


def dense_block(tiles, where):
    slots = tiles.shape[0]
    cells = 256
    half = jax.ShapeDtypeStruct((16 * E, 8 * E), BF)
    spec = pl.BlockSpec((E, 8 * E), lambda i, where: (i, 0))
    return pl.pallas_call(
        lambda *refs: dense_kernel(slots, cells, *refs),
        out_shape=(half, half),
        grid_spec=pltpu.PrefetchScalarGridSpec(
            num_scalar_prefetch=1,
            grid=(16,),
            in_specs=[pl.BlockSpec(memory_space=pl.ANY)],
            out_specs=[spec, spec],
            scratch_shapes=[
                pltpu.VMEM((slots, E, E), BF),
                pltpu.SMEM((cells + 1,), jnp.int32),
                pltpu.SMEM((slots,), jnp.int32),
                pltpu.SemaphoreType.DMA(()),
            ],
        ),
        compiler_params=pltpu.CompilerParams(vmem_limit_bytes=16 << 20),
        name="dense_block",
    )(where, tiles)


def body(features, weight, history, in_batch, tile_values, tile_pos, tile_count, cotangent):
    nodes = features.shape[0] * lax.axis_size("row") * lax.axis_size("col")
    width = weight.shape[1]
    row = lax.axis_index("row")
    col = lax.axis_index("col")
    tiles = tile_values.reshape(tile_values.shape[2:])
    coords = tile_pos.reshape(tile_pos.shape[2], 2)
    count = tile_count.reshape(())

    trow, tcol = coords[:, 0], coords[:, 1]
    rel_core = (trow ^ col) & 1
    rel_z = ((trow >> 1) - (col >> 1)) & 3
    rel_x = ((trow >> 3) - (col >> 3)) & 3
    rel_half = (tcol ^ row) & 1
    rel_y = ((tcol >> 1) - (row >> 1)) & 3
    where = (rel_core * 16 + rel_x * 4 + rel_z) * 8 + rel_y * 2 + rel_half
    where = jnp.where(jnp.arange(where.shape[0], dtype=jnp.int32) < count, where, 256).astype(jnp.int32)

    chosen = in_batch[:, None] == 1
    projected = jnp.dot(features, weight, preferred_element_type=F32).astype(BF)
    mixed = jnp.where(chosen, projected, history)
    masked = jnp.where(chosen, features, jnp.zeros_like(features))

    def row_panel(value):
        pair = jnp.concatenate([value, shift(value, "half")])
        return jnp.concatenate(gather_ring(pair, "y"))

    panel = row_panel(mixed)
    a_near, a_far = dense_block(tiles, where)

    far = jnp.dot(a_far, panel, preferred_element_type=F32).astype(BF)
    far_got = shift(far, "core")
    near = jnp.dot(a_near, panel, preferred_element_type=F32)
    rows = near + far_got.astype(F32)
    q = 4 * E
    quarter = reduce_ring([rows[i * q:(i + 1) * q] for i in range(4)], "x")
    total = reduce_ring([quarter[i * E:(i + 1) * E] for i in range(4)], "z")

    output = gelu_form(total).astype(BF)
    _, pullback = jax.vjp(gelu_form, total)
    grad_total = pullback(cotangent.astype(F32))[0].astype(BF)

    grad_quarter = jnp.concatenate(gather_ring(grad_total, "z"))
    grad_near = jnp.concatenate(gather_ring(grad_quarter, "x"))
    grad_far = shift(grad_near, "core")
    masked_late, _ = lax.optimization_barrier((masked, far))
    masked_panel = row_panel(masked_late)

    dims = (((0,), (0,)), ((), ()))
    part = lax.dot_general(a_near, grad_near, dims, preferred_element_type=F32)
    part = part + lax.dot_general(a_far, grad_far, dims, preferred_element_type=F32)
    wpart = lax.dot_general(masked_panel, part.astype(BF), dims, preferred_element_type=F32)

    wrows = wpart.reshape(4, 2, 16, width)
    wrows = jnp.concatenate([wrows, wrows])
    wrows = lax.dynamic_slice_in_dim(wrows, row >> 1, 4, 0)
    wmine = lax.dynamic_slice_in_dim(jnp.concatenate([wrows, wrows], axis=1), row & 1, 2, 1)
    part = part.reshape(4, 2, E, width)
    joined = jnp.concatenate([part, wmine], axis=2).reshape(4, 2 * (E + 16), width)
    pair = reduce_ring([joined[i] for i in range(4)], "y")
    block = E + 16
    summed = pair[:block] + shift(pair[block:].astype(BF), "half").astype(F32)

    grad_projected = jnp.where(chosen, summed[:E], 0.0).astype(BF)
    grad_features = lax.dot_general(
        grad_projected, weight, (((1,), (1,)), ((), ())), preferred_element_type=F32
    ).astype(BF)

    w = summed[E:]
    w = w + xor_col(w, 1)
    w = (w + xor_col(w, 8)) + (xor_col(w, 16) + xor_col(w, 24))
    w = (w + xor_col(w, 2)) + (xor_col(w, 4) + xor_col(w, 6))
    w = w * F32(1.0 / math.sqrt(nodes))
    pieces = jnp.stack([w] + [xor_row(w, m) for m in range(1, 8)])
    order = jnp.arange(8, dtype=jnp.int32) ^ row
    grad_weight = pieces[order].reshape(E, width)
    return (output, grad_features, grad_weight)


def solution(mesh):
    in_specs = (
        P(("col", "row"), None),
        P(),
        P(("col", "row"), None),
        P(("col", "row")),
        P("row", "col", None, None, None),
        P("row", "col", None, None),
        P("row", "col"),
        P(("row", "col"), None),
    )
    out_specs = (P(("row", "col"), None), P(("col", "row"), None), P())
    return jax.shard_map(body, mesh=mesh, in_specs=in_specs, out_specs=out_specs, check_vma=False)
```

```python
import math

import jax
import jax.numpy as jnp
from jax import lax
from jax.experimental import pallas as pl
from jax.experimental.pallas import tpu as pltpu
from jax.sharding import PartitionSpec as P


BF = jnp.bfloat16
F32 = jnp.float32
E = 128


def gelu_form(values):
    return jax.nn.gelu(values, approximate=True)


MASKS = {"x": ("col", 8), "z": ("col", 2), "core": ("col", 1), "y": ("row", 2), "half": ("row", 1)}


def trade(value, axis, k):
    over, unit = MASKS[axis]
    return swap(value, over, unit * k)


def swap(value, axis, mask):
    size = lax.axis_size(axis)
    return lax.ppermute(value, axis, [(dev, dev ^ mask) for dev in range(size)])


def dense_kernel(slots, where_ref, tiles_hbm, near_ref, far_ref, tiles, head, link, sem):
    step = pl.program_id(0)

    @pl.when(step == 0)
    def _():
        copy = pltpu.make_async_copy(tiles_hbm, tiles.at[pl.ds(0, slots)], sem)
        copy.start()
        tiles[slots] = jnp.zeros((E, E), BF)

        def clear(i, carry):
            head[i] = slots
            return carry

        lax.fori_loop(0, 264, clear, 0, unroll=8)
        link[slots] = slots

        def insert(s, carry):
            at = where_ref[s]
            link[s] = head[at]
            head[at] = s
            return carry

        lax.fori_loop(0, slots, insert, 0, unroll=4)
        copy.wait()

    for out_ref, base in ((near_ref, 0), (far_ref, 128)):
        firsts = [head[base + step * 8 + c] for c in range(8)]
        for c in range(8):
            out_ref[:, c * E:(c + 1) * E] = tiles[firsts[c]]
        for c in range(8):
            second = link[firsts[c]]

            @pl.when(second < slots)
            def _(out_ref=out_ref, c=c, first=firsts[c], second=second):
                def more(state):
                    return state[0] < slots

                def add(state):
                    at, acc = state
                    return link[at], acc + tiles[at].astype(F32)

                _, acc = lax.while_loop(more, add, (second, tiles[first].astype(F32)))
                out_ref[:, c * E:(c + 1) * E] = acc.astype(BF)


def dense_block(tiles, where):
    slots = tiles.shape[0]
    half = jax.ShapeDtypeStruct((16 * E, 8 * E), BF)
    spec = pl.BlockSpec((E, 8 * E), lambda i, where: (i, 0))
    return pl.pallas_call(
        lambda *refs: dense_kernel(slots, *refs),
        out_shape=(half, half),
        grid_spec=pltpu.PrefetchScalarGridSpec(
            num_scalar_prefetch=1,
            grid=(16,),
            in_specs=[pl.BlockSpec(memory_space=pltpu.HBM)],
            out_specs=[spec, spec],
            scratch_shapes=[
                pltpu.VMEM((slots + 1, E, E), BF),
                pltpu.SMEM((264,), jnp.int32),
                pltpu.SMEM((slots + 1,), jnp.int32),
                pltpu.SemaphoreType.DMA(()),
            ],
        ),
        compiler_params=pltpu.CompilerParams(vmem_limit_bytes=16 << 20),
        name="dense_block",
    )(where, tiles)


def layer(features, weight, history, in_batch, tile_values, tile_pos, tile_count, cotangent):
    nodes = features.shape[0] * lax.axis_size("row") * lax.axis_size("col")
    width = weight.shape[1]
    row = lax.axis_index("row")
    col = lax.axis_index("col")
    tiles = pltpu.with_memory_space_constraint(tile_values.reshape(tile_values.shape[2:]), pltpu.HBM)
    coords = tile_pos.reshape(tile_pos.shape[2], 2)
    count = tile_count.reshape(())

    trow, tcol = coords[:, 0], coords[:, 1]
    rel_core = (trow ^ col) & 1
    rel_z = ((trow ^ col) >> 1) & 3
    rel_x = ((trow ^ col) >> 3) & 3
    rel_x = rel_x ^ (rel_x >> 1)
    where = (rel_core * 16 + rel_x * 4 + rel_z) * 8 + tcol
    where = jnp.where(jnp.arange(where.shape[0], dtype=jnp.int32) < count, where, 256).astype(jnp.int32)

    chosen = in_batch[:, None] == 1
    projected = jnp.dot(features, weight, preferred_element_type=F32).astype(BF)
    mixed = jnp.where(chosen, projected, history)
    masked = jnp.where(chosen, features, jnp.zeros_like(features))
    own = jnp.concatenate([mixed, masked], axis=1)

    other = trade(own, "half", 1)
    low = row & 1
    pair = jnp.concatenate([jnp.where(low == 0, own, other), jnp.where(low == 0, other, own)])
    panel = jnp.zeros((8 * E, pair.shape[1]), BF)
    y = row >> 1
    pairs = [(2, trade(pair, "y", 2)), (1, trade(pair, "y", 1)), (3, trade(pair, "y", 3)), (0, pair)]
    for step, got in pairs:
        panel = lax.dynamic_update_slice(panel, got, ((y ^ step) * 2 * E, 0))
    a_near, a_far = dense_block(tiles, where)

    q = 4 * E
    far_two = jnp.dot(a_far[3 * q:], panel, preferred_element_type=F32).astype(BF)
    got_two = trade(far_two, "core", 1)
    far = jnp.dot(a_far[:3 * q], panel, preferred_element_type=F32).astype(BF)
    got_rest = trade(far, "core", 1)
    near = jnp.dot(a_near, panel, preferred_element_type=F32)
    two = (near[3 * q:] + got_two.astype(F32)).astype(BF)
    h = q // 2
    half_a = trade(two[:h], "x", 1)
    half_b = trade(two[h:], "x", 3)
    rest = near[:3 * q] + got_rest.astype(F32)
    one_a = trade(rest[q:q + h].astype(BF), "x", 1)
    three_b = trade(rest[2 * q + h:].astype(BF), "x", 3)
    three_a = trade((rest[2 * q:2 * q + h] + half_a.astype(F32)).astype(BF), "x", 3)
    one_b = trade((rest[q + h:2 * q] + half_b.astype(F32)).astype(BF), "x", 1)
    one_a, one_b, three_a, three_b = lax.optimization_barrier((one_a, one_b, three_a, three_b))
    quarter = jnp.concatenate([
        rest[:h] + (one_a.astype(F32) + three_a.astype(F32)),
        rest[h:q] + (one_b.astype(F32) + three_b.astype(F32)),
    ])
    sent = quarter.astype(BF)
    total = quarter[:E]
    for k in (1, 2, 3):
        total = total + trade(sent[k * E:(k + 1) * E], "z", k).astype(F32)
    feature_rows = total[:, width:].astype(BF)
    total = total[:, :width]

    output = gelu_form(total).astype(BF)
    _, pullback = jax.vjp(gelu_form, total)
    grad_total = pullback(cotangent.astype(F32))[0].astype(BF)
    dims = (((0,), (0,)), ((), ()))
    w = lax.dot_general(feature_rows, grad_total, dims, preferred_element_type=F32)

    own_q = [grad_total] + [trade(grad_total, "z", k) for k in (1, 2, 3)]
    own_q = jnp.concatenate(own_q)
    three_a = trade(own_q[:h], "x", 3)
    one_b = trade(own_q[h:], "x", 1)
    one_a = trade(own_q[:h], "x", 1)
    three_b = trade(own_q[h:], "x", 3)
    far_0 = trade(own_q, "core", 1)
    far_1 = trade(three_a, "x", 1)
    far_2 = trade(one_b, "x", 3)
    near_13 = jnp.concatenate([one_a, one_b, three_a, three_b])
    far_13 = trade(near_13, "core", 1)
    near_2 = jnp.concatenate([far_1, far_2])
    far_22 = trade(near_2, "core", 1)
    grad_near = jnp.concatenate([own_q, near_13, near_2])
    grad_far = jnp.concatenate([far_0, far_13, far_22])

    part = lax.optimization_barrier(lax.dot_general(a_near, grad_near, dims, preferred_element_type=F32))
    part = (part + lax.dot_general(a_far, grad_far, dims, preferred_element_type=F32)).astype(BF)
    parts = lax.all_to_all(part.reshape(8, E, width), "row", 0, 0, tiled=True)

    bit = col & 1
    w = w.reshape(2, w.shape[0] // 2, width)
    keep = lax.dynamic_index_in_dim(w, bit, 0, False)
    w = keep + swap(lax.dynamic_index_in_dim(w, 1 - bit, 0, False), "col", 1)
    steps = (("row", 2), ("row", 6), ("row", 1), ("col", 2), ("col", 6), ("col", 8), ("col", 24))
    for axis, mask in steps:
        w = w + swap(w, axis, mask)
    w = w * F32(1.0 / math.sqrt(nodes))
    got = swap(w, "col", 1)
    w = jnp.concatenate([jnp.where(bit == 0, w, got), jnp.where(bit == 0, got, w)])

    grad_mixed = jnp.sum(parts.astype(F32), axis=0)
    grad_projected = jnp.where(chosen, grad_mixed, 0.0).astype(BF)
    grad_features = lax.dot_general(
        grad_projected, weight, (((1,), (1,)), ((), ())), preferred_element_type=F32
    ).astype(BF)
    return (output, grad_features, w)


def solution(mesh):
    in_specs = (
        P(("col", "row"), None),
        P(),
        P(("col", "row"), None),
        P(("col", "row")),
        P("row", "col", None, None, None),
        P("row", "col", None, None),
        P("row", "col"),
        P(("row", "col"), None),
    )
    out_specs = (P(("row", "col"), None), P(("col", "row"), None), P())
    return jax.shard_map(layer, mesh=mesh, in_specs=in_specs, out_specs=out_specs, check_vma=False)
```
